32 devices in a mesh: groups: 1, wide: 8 (over y, x, core), narrow: 4 (over z).
Axes of the slice: x: 2, y: 2, z: 4, core: 2. Of those that a mesh axis runs over, the one named last changes fastest.
Arguments:
- table_cells: bfloat16 [128, 128, 192], P(('groups', 'wide', 'narrow')), may hold values from -12 to 12
- counts: int32 [128], P(('groups', 'wide', 'narrow')), may hold values from 32 to 128, as said below
- train_count: int32 [1], P('groups'), may hold values from 32 to 96
- norm_gain: float32 [3, 192], replicated, may hold values from 0.5 to 1.5
- feature_in: bfloat16 [192, 576], P('narrow'), may hold values from -0.4375 to 0.4375
- feature_out: bfloat16 [192, 192], P('narrow'), may hold values from -0.4375 to 0.4375
- sample_in: bfloat16 [192, 576], P('narrow'), may hold values from -0.4375 to 0.4375
- sample_out: bfloat16 [192, 192], P('narrow'), may hold values from -0.4375 to 0.4375
- hidden_up: bfloat16 [192, 768], P('narrow'), may hold values from -0.4375 to 0.4375
- hidden_down: bfloat16 [768, 192], P('narrow'), may hold values from -0.21875 to 0.21875
Outputs:
- updated_cells: bfloat16 [128, 128, 192], P(('groups', 'wide', 'narrow'))
The draws below stay inside these ranges and needn't reach their ends.
Inputs may be any that keep to these rules, and one draw needn't show every extreme that they name: `counts`: feature j of a row is present when j < its count; some row has all 128 features present. Rows 0 to train_count - 1 are the training rows.
All inputs are finite; a program needn't handle non-finite values.
Results may differ from the reference program's by a relative error of at most 0.0086.
Values may be sent and summed in bfloat16 or wider, within the bound.
A program may use at most 64 MiB of HBM per device.

```python
import jax
import jax.numpy as jnp
from jax import lax

E = 192
HEADS = 6
HIDDEN_UNITS = 768
ROWS = 128
FEATS = 128


def draw_table_cells(key, part):
    values = jax.random.normal(key, (ROWS, FEATS, E), jnp.float32)
    return jnp.clip(values, -12.0, 12.0).astype(jnp.bfloat16)


def draw_counts(key, part):
    drawn = jax.random.randint(jax.random.fold_in(key, 11), (ROWS,), FEATS // 4, FEATS + 1).astype(jnp.int32)
    return drawn.at[0].set(FEATS)


def shard_levels(key, dims, cuts, smallest, top_value):
    factor_of = 1.0
    for dim, blocks in cuts:
        draws = jax.random.uniform(jax.random.fold_in(jax.random.fold_in(key, 6), dim), (blocks,), jnp.float32, smallest / len(cuts), top_value / len(cuts))
        factor_of = factor_of * jnp.repeat(jnp.exp(draws), dims[dim] // blocks).reshape((-1,) + (1,) * (len(dims) - 1 - dim))
    return factor_of


def noise(rng, extent, scale, bound, shards=(), dtype=jnp.bfloat16):
    values = scale * jax.random.normal(rng, extent, jnp.float32)
    if shards:
        values = values * shard_levels(rng, extent, shards, -0.22, 0.18)
    return jnp.clip(values, -bound, bound).astype(dtype)


def setup_inputs(seed: int = 0, part: int = 0) -> dict:
    key_of = jax.random.split(jax.random.key(seed), 11)
    part_keys = jax.random.split(jax.random.fold_in(key_of[10], part), 11)
    table_cells = draw_table_cells(jax.random.fold_in(jax.random.fold_in(key_of[10], part), 71), part)
    counts = draw_counts(jax.random.fold_in(jax.random.fold_in(key_of[10], part), 71), part)
    train_count = jax.random.randint(part_keys[2], (1,), ROWS // 4, 3 * ROWS // 4 + 1).astype(jnp.int32)
    norm_gain = jnp.clip(1.0 + 0.1 * jax.random.normal(key_of[3], (3, E), jnp.float32), 0.5, 1.5)
    feature_in = noise(key_of[4], (E, 3 * E), E ** -0.5, 0.4375, ((0, 4),))
    feature_out = noise(key_of[5], (E, E), E ** -0.5, 0.4375, ((0, 4),))
    sample_in = noise(key_of[6], (E, 3 * E), E ** -0.5, 0.4375, ((0, 4),))
    sample_out = noise(key_of[7], (E, E), E ** -0.5, 0.4375, ((0, 4),))
    hidden_up = noise(key_of[8], (E, HIDDEN_UNITS), E ** -0.5, 0.4375, ((0, 4),))
    hidden_down = noise(key_of[9], (HIDDEN_UNITS, E), HIDDEN_UNITS ** -0.5, 0.21875, ((0, 4),))
    return {"table_cells": table_cells, "counts": counts, "train_count": train_count, "norm_gain": norm_gain, "feature_in": feature_in, "feature_out": feature_out, "sample_in": sample_in, "sample_out": sample_out, "hidden_up": hidden_up, "hidden_down": hidden_down}


epsilon = 1e-05

def normalize(values, gain):
    average = lax.optimization_barrier(jnp.mean(values, axis=-1, keepdims=True))
    centered = values - average
    spread = lax.optimization_barrier(jnp.mean(centered * centered, axis=-1, keepdims=True))
    return centered * lax.rsqrt(spread + epsilon) * gain

def attend(packed, valid, head_count):
    length = packed.shape[0]
    model_width = packed.shape[1] // 3
    head_size = model_width // head_count
    queries = packed[:, :model_width].reshape(length, head_count, head_size).astype(jnp.float32)
    key_part = packed[:, model_width:2 * model_width].reshape(length, head_count, head_size).astype(jnp.float32)
    value_part = packed[:, 2 * model_width:].reshape(length, head_count, head_size).astype(jnp.float32)
    scores = jnp.einsum('qhd,khd->hqk', queries, key_part) * (1.0 / jnp.sqrt(jnp.float32(head_size)))
    scores = jnp.where(valid[None, None, :], scores, jnp.float32(-1e+30))
    maxima = lax.optimization_barrier(jnp.max(scores, axis=-1, keepdims=True))
    exponentials = jnp.where(valid[None, None, :], jnp.exp(scores - maxima), jnp.float32(0.0))
    totals = lax.optimization_barrier(jnp.sum(exponentials, axis=-1, keepdims=True))
    probabilities = (exponentials / totals).astype(jnp.bfloat16)
    context = jnp.einsum('hqk,khd->qhd', probabilities.astype(jnp.float32), value_part)
    return context.reshape(length, model_width).astype(jnp.bfloat16)

def reference(table_cells, counts, train_count, norm_gain, feature_in, feature_out, sample_in, sample_out, hidden_up, hidden_down):
    feature_ids = jnp.arange(FEATS).astype(jnp.int32)
    row_ids = jnp.arange(ROWS).astype(jnp.int32)

    def feature_row(pair):
        row_cells, count = pair
        packed = jnp.dot(row_cells, feature_in, preferred_element_type=jnp.float32).astype(jnp.bfloat16)
        context = attend(packed, feature_ids < count, HEADS)
        update = jnp.dot(context, feature_out, preferred_element_type=jnp.float32)
        return normalize(row_cells.astype(jnp.float32) + update, norm_gain[0]).astype(jnp.bfloat16)
    first = lax.map(feature_row, (table_cells, counts))
    columns = jnp.swapaxes(first, 0, 1)
    valid = row_ids < train_count[0]

    def sample_column(column):
        packed = jnp.dot(column, sample_in, preferred_element_type=jnp.float32).astype(jnp.bfloat16)
        context = attend(packed, valid, HEADS)
        update = jnp.dot(context, sample_out, preferred_element_type=jnp.float32)
        second = normalize(column.astype(jnp.float32) + update, norm_gain[1]).astype(jnp.bfloat16)
        hidden = jax.nn.gelu(jnp.dot(second, hidden_up, preferred_element_type=jnp.float32), approximate=False).astype(jnp.bfloat16)
        back = jnp.dot(hidden, hidden_down, preferred_element_type=jnp.float32)
        return normalize(second.astype(jnp.float32) + back, norm_gain[2]).astype(jnp.bfloat16)
    result = lax.map(sample_column, columns)
    return jnp.swapaxes(result, 0, 1)
```

```python
import functools
import math

import jax
import jax.numpy as jnp
from jax import lax
from jax.experimental import pallas as pl
from jax.experimental.pallas import tpu as pltpu
from jax.sharding import PartitionSpec as P

HEADS = 6
EPSILON = 1e-05
MESH = pl.DeviceIdType.MESH
F32 = jnp.float32
BF16 = jnp.bfloat16


def normalize(values, gain):
    average = jnp.mean(values, axis=-1, keepdims=True)
    centered = values - average
    spread = jnp.mean(centered * centered, axis=-1, keepdims=True)
    return centered * lax.rsqrt(spread + EPSILON) * gain


def matmul(a, b):
    return jnp.dot(a, b, preferred_element_type=F32)


def gathered(ref, part):
    parts, _, rows, columns = ref.shape
    if rows % 16 == 0:
        return ref[:, part].reshape(parts * rows, columns)
    pieces = [ref[i, part].astype(F32) for i in range(parts)]
    return jnp.concatenate(pieces, axis=0).astype(BF16)


def gathered_down(ref, width):
    pieces = []
    for owner in range(ref.shape[0]):
        for part in (2, 3):
            both = ref[owner, part].astype(F32)
            pieces += [both[:, :width], both[:, width:]]
    return jnp.concatenate(pieces, axis=0).astype(BF16)


def one_hot(count, depth, start, source):
    to = lax.broadcasted_iota(jnp.int32, (count, 1), 0) + start
    column = lax.broadcasted_iota(jnp.int32, (count, depth), 1)
    return jnp.where(column == source(to), 1.0, 0.0).astype(BF16)


def prepare(ref, source, chunk=512):
    count, depth = ref.shape
    chunk = min(chunk, count)
    for start in range(0, count, chunk):
        ref[start : start + chunk, :] = one_hot(chunk, depth, start, source)


def reorder(pick, x, start=0, count=None, chunk=512):
    count = pick.shape[0] if count is None else count
    chunk = min(chunk, count)
    pieces = [
        matmul(pick[at : at + chunk, :], x) for at in range(start, start + count, chunk)
    ]
    return pieces[0] if len(pieces) == 1 else jnp.concatenate(pieces, axis=0)


def attend(q, k, v, bias, ones):
    length, width = q.shape
    head_size = width // HEADS
    factor = math.log2(math.e) / math.sqrt(head_size)
    head_of = lax.broadcasted_iota(jnp.int32, (length, width), 1) // head_size
    zero = jnp.zeros_like(k)
    masks = [head_of == h for h in range(HEADS)]
    keys = jnp.concatenate([jnp.where(m, k, zero) for m in masks], axis=0)
    values = jnp.concatenate([jnp.where(m, v, zero) for m in masks], axis=0)
    scores = lax.dot_general(q, keys, (((1,), (1,)), ((), ())), preferred_element_type=F32)
    powers = []
    for h in range(HEADS):
        s = scores[:, h * length : (h + 1) * length] * factor + bias
        powers.append(jnp.exp2(s - jnp.max(s, axis=-1, keepdims=True)).astype(BF16))
    weight = jnp.concatenate(powers, axis=1)
    return (matmul(weight, values) / matmul(weight, ones)).astype(BF16)


def head_ones(ref, length):
    row = lax.broadcasted_iota(jnp.int32, ref.shape, 0) // length
    lane = lax.broadcasted_iota(jnp.int32, ref.shape, 1) // (ref.shape[1] // HEADS)
    ref[...] = jnp.where(row == lane, 1.0, 0.0).astype(BF16)


def attention_block(x, left, right, qkv_ref, ctx_ref, ones_ref, length, bias_of, gain):
    width = x.shape[1]
    qk = matmul(x, left).astype(BF16)
    qkv_ref[0] = qk[:, :width]
    qkv_ref[1] = qk[:, width:]
    qkv_ref[2] = matmul(x, right[:, :width]).astype(BF16)

    def one(i):
        rows = pl.ds(pl.multiple_of(i * length, length), length)
        ctx_ref[rows, :] = attend(
            qkv_ref[0, rows, :], qkv_ref[1, rows, :], qkv_ref[2, rows, :], bias_of(i), ones_ref[...]
        )

    count = x.shape[0] // length
    if length <= 128:
        for i in range(count):
            one(i)
    else:
        pl.loop(0, count)(one)
    update = matmul(ctx_ref[...], right[:, width:])
    return normalize(x.astype(F32) + update, gain).astype(BF16)


def kernel(
    sizes,
    counts_hbm,
    train_hbm,
    gain_hbm,
    cells_hbm,
    fi_hbm,
    fo_hbm,
    si_hbm,
    so_hbm,
    hu_hbm,
    hd_hbm,
    out_hbm,
    counts_ref,
    train_ref,
    gain_ref,
    cells_ref,
    x_ref,
    fi_ref,
    fo_ref,
    si_ref,
    so_ref,
    hu_ref,
    hd_ref,
    wf,
    ws,
    wb,
    qkv,
    ctx,
    pick_send,
    pick_column,
    pick_row,
    feature_ones,
    sample_ones,
    send1,
    recv1,
    send2,
    recv2,
    ready,
    sa,
    ra,
    sb,
    rb,
    sz,
    rz,
    sp,
    sm,
    rm,
    cell_sems,
    load_sems,
    out_sems,
):
    wide, narrow = sizes
    total = wide * narrow
    chips = wide // 2
    g = lax.axis_index("groups")
    w = lax.axis_index("wide")
    n = lax.axis_index("narrow")
    me = w * narrow + n
    core = lax.rem(w, 2)
    chip = w // 2
    mate = w + 1 - 2 * core
    rows, width, feats = cells_ref.shape
    local = feats // total
    hl = local // 2
    pair = rows // 2
    piece = pair * hl
    all_rows = rows * total
    half_cells = rows * feats // 2

    barrier = pltpu.get_barrier_semaphore()
    for step in range(1, narrow):
        pl.semaphore_signal(
            barrier, inc=1, device_id=(g, w, lax.rem(n + step, narrow)), device_id_type=MESH
        )
    for step in range(1, wide):
        pl.semaphore_signal(
            barrier, inc=1, device_id=(g, lax.rem(w + step, wide), n), device_id_type=MESH
        )

    loads = [
        pltpu.make_async_copy(src, dst, load_sems.at[i])
        for i, (src, dst) in enumerate(
            (
                (fi_hbm, fi_ref),
                (fo_hbm, fo_ref),
                (cells_hbm, cells_ref),
                (si_hbm, si_ref),
                (so_hbm, so_ref),
                (hu_hbm, hu_ref),
                (hd_hbm, hd_ref),
                (gain_hbm, gain_ref),
                (counts_hbm, counts_ref),
                (train_hbm, train_ref),
            )
        )
    ]
    for load in loads:
        load.start()
    double = 2 * width
    shard = fi_ref.shape[0]
    loads[0].wait()
    loads[1].wait()
    wf[n, 0] = fi_ref[:, :double]
    wf[n, 1] = jnp.concatenate([fi_ref[:, double:], fo_ref[...]], axis=1)
    pl.semaphore_wait(barrier, narrow - 1 + wide - 1)

    weights = (wf, ws)
    steps = range(1, narrow)

    def along(group, step):
        ref = weights[group]
        return pltpu.make_async_remote_copy(
            src_ref=ref.at[n, core],
            dst_ref=ref.at[n, core],
            send_sem=sa.at[group, step],
            recv_sem=ra.at[group, step],
            device_id=(g, w, lax.rem(n + step, narrow)),
            device_id_type=MESH,
        )

    def across(group, step):
        ref = weights[group]
        owner = lax.rem(n - step + narrow, narrow)
        return pltpu.make_async_remote_copy(
            src_ref=ref.at[owner, core],
            dst_ref=ref.at[owner, core],
            send_sem=sb.at[group, step],
            recv_sem=rb.at[group, step],
            device_id=(g, mate, n),
            device_id_type=MESH,
        )

    def big(slot, step):
        block = core + 2 * slot
        return pltpu.make_async_remote_copy(
            src_ref=wb.at[n, block],
            dst_ref=wb.at[n, block],
            send_sem=sz.at[slot, step],
            recv_sem=rz.at[slot, step],
            device_id=(g, w, lax.rem(n + step, narrow)),
            device_id_type=MESH,
        )

    def spread(slot, step, to):
        block = core + 2 * slot
        owner = lax.rem(n - step + narrow, narrow)
        return pltpu.make_async_remote_copy(
            src_ref=wb.at[owner, block],
            dst_ref=wb.at[owner, block],
            send_sem=sp.at[slot, step, to],
            recv_sem=rz.at[slot, step],
            device_id=(g, lax.rem(w + 2 * to, wide), n),
            device_id_type=MESH,
        )

    def shared(slot, step):
        block = core + 2 * slot
        owner = lax.rem(n - step + narrow, narrow)
        return pltpu.make_async_remote_copy(
            src_ref=wb.at[owner, block],
            dst_ref=wb.at[owner, block],
            send_sem=sm.at[slot, step],
            recv_sem=rm.at[slot, step],
            device_id=(g, mate, n),
            device_id_type=MESH,
        )

    for step in steps:
        along(0, step).start()
    for step in steps:
        pl.semaphore_signal(
            ready, inc=1, device_id=(g, w, lax.rem(n + step, narrow)), device_id_type=MESH
        )

    for load in loads[3:7]:
        load.wait()
    ws[n, 0] = si_ref[:, :double]
    ws[n, 1] = jnp.concatenate([si_ref[:, double:], so_ref[...]], axis=1)
    wb[n, 0] = hu_ref[:, :double]
    wb[n, 1] = hu_ref[:, double:]
    down = hd_ref[...].astype(F32)
    for i in range(2):
        top = down[2 * i * shard : (2 * i + 1) * shard]
        low = down[(2 * i + 1) * shard : (2 * i + 2) * shard]
        wb[n, 2 + i] = jnp.concatenate([top, low], axis=1).astype(BF16)
    loads[2].wait()
    for r in range(rows):
        x_ref[r * feats : (r + 1) * feats, :] = cells_ref[r].astype(F32).T.astype(BF16)

    def to_send(i):
        h, k = i // (half_cells // 2), i % (half_cells // 2)
        d, r, j = k // piece, (k % piece) // hl, k % hl
        return r * feats + d * local + h * hl + j

    def to_column(i):
        j, k = i // all_rows, i % all_rows
        s, r = k // rows, k % rows
        return (r // pair) * (total * piece) + s * piece + (r % pair) * hl + j

    def to_row(j):
        def source(i):
            r, f = i // feats, i % feats
            d, h, at = f // local, (f % local) // hl, f % hl
            k = h * all_rows + d * rows + r
            return jnp.where(at == j, k, -1)

        return source

    prepare(pick_send, to_send)
    prepare(pick_column, to_column)
    for j in range(hl):
        prepare(pick_row.at[j], to_row(j))
    head_ones(feature_ones, feats)
    head_ones(sample_ones, all_rows)
    for load in loads[7:]:
        load.wait()

    for step in steps:
        along(0, step).wait_recv()
        across(0, step).start()
    for step in steps:
        along(1, step).start()
    for slot in range(2):
        @pl.when(chip == core + 2 * slot)
        def _(slot=slot):
            for step in steps:
                big(slot, step).start()
    for step in steps:
        across(0, step).wait_recv()

    near = [(a, b) for b in range(narrow) for a in range(wide) if a or b]
    near.sort(key=lambda t: (-min(t[1], narrow - t[1]), -min(t[0], wide - t[0])))

    def copy_to(send, recv, index, part, a, b):
        tw, tn = lax.rem(w + a, wide), lax.rem(n + b, narrow)
        return pltpu.make_async_remote_copy(
            src_ref=send.at[part, tw * narrow + tn],
            dst_ref=recv.at[part, me],
            send_sem=cell_sems.at[index, 0, part],
            recv_sem=cell_sems.at[index, 1, part],
            device_id=(g, tw, tn),
            device_id_type=MESH,
        )

    def exchange(send, recv, index, part):
        recv[part, me] = send[part, me]
        if total <= 32:
            for a, b in near:
                copy_to(send, recv, index, part, a, b).start()
        else:
            @pl.loop(1, total)
            def _(step):
                copy_to(send, recv, index, part, step // narrow, lax.rem(step, narrow)).start()

    def exchanged(ref, index, way, part):
        whole = ref.at[part, pl.ds(0, total - 1)]
        pltpu.make_async_copy(whole, whole, cell_sems.at[index, way, part]).wait()

    keys = lax.broadcasted_iota(jnp.int32, (1, feats), 1)
    left, right = gathered(wf, 0), gathered(wf, 1)
    for q in range(2):
        x = x_ref[q * half_cells : (q + 1) * half_cells, :]
        first = attention_block(
            x,
            left,
            right,
            qkv,
            ctx,
            feature_ones,
            feats,
            lambda i: jnp.where(keys < counts_ref[q * pair + i], 0.0, -1e30),
            gain_ref[0:1, :],
        )
        picked = reorder(pick_send, first)
        both = jnp.concatenate([picked[: half_cells // 2], picked[half_cells // 2 :]], axis=1)
        send1[q] = both.reshape(total, piece, double).astype(BF16)
        if q == 0:
            pl.semaphore_wait(ready, narrow - 1)
        exchange(send1, recv1, 0, q)

    for step in steps:
        along(1, step).wait_recv()
        across(1, step).start()
    for slot in range(2):
        @pl.when(chip == core + 2 * slot)
        def _(slot=slot):
            for step in steps:
                big(slot, step).wait_recv()
                for to in range(1, chips):
                    spread(slot, step, to).start()
                shared(slot, step).start()
    for slot in range(2):
        @pl.when(chip != core + 2 * slot)
        def _(slot=slot):
            for step in steps:
                big(slot, step).wait_recv()
                shared(slot, step).start()
    for step in steps:
        across(1, step).wait_recv()
    left, right = gathered(ws, 0), gathered(ws, 1)
    for q in range(2):
        exchanged(recv1, 0, 1, q)

    samples = lax.broadcasted_iota(jnp.int32, (1, all_rows), 1)
    sample_bias = jnp.where(samples < train_ref[0], 0.0, -1e30)
    landed = jnp.concatenate(
        [recv1[q].astype(F32).reshape(total * piece, double).astype(BF16) for q in range(2)], axis=0
    )
    tile = min(512, half_cells)
    for j in range(hl):
        y = reorder(pick_column, landed, j * all_rows, all_rows).astype(BF16)
        y = jnp.concatenate([y[:, :width], y[:, width:]], axis=0)
        second = attention_block(
            y, left, right, qkv, ctx, sample_ones, all_rows, lambda i: sample_bias, gain_ref[1:2, :]
        )
        ctx[...] = second
        if j == 0:
            for step in steps:
                for slot in range(2):
                    shared(slot, step).wait_recv()
            up = [gathered(wb, c) for c in range(2)]
            low = gathered_down(wb, width)

        def feed(i):
            at = pl.ds(pl.multiple_of(i * tile, tile), tile)
            values = ctx[at, :]
            halves = []
            for c in range(2):
                h = matmul(values, up[c])
                halves.append((0.5 * h * (1.0 + lax.erf(h * (2.0**-0.5)))).astype(BF16))
            back = matmul(jnp.concatenate(halves, axis=1), low)
            ctx[at, :] = normalize(values.astype(F32) + back, gain_ref[2:3, :]).astype(BF16)

        if half_cells == tile:
            feed(0)
        else:
            pl.loop(0, half_cells // tile)(feed)
        done = jnp.concatenate([ctx[:all_rows, :], ctx[all_rows:, :]], axis=1)
        send2[j] = done.astype(F32).reshape(total, rows, double).astype(BF16)
        exchange(send2, recv2, 1, j)

    for step in steps:
        for group in range(2):
            along(group, step).wait_send()
            across(group, step).wait_send()
        for slot in range(2):
            @pl.when(chip == core + 2 * slot)
            def _(slot=slot, step=step):
                big(slot, step).wait_send()
                for to in range(1, chips):
                    spread(slot, step, to).wait_send()

            shared(slot, step).wait_send()
    for q in range(2):
        exchanged(send1, 0, 0, q)

    parts = []
    for j in range(hl):
        exchanged(recv2, 1, 1, j)
        both = recv2[j].astype(F32).reshape(all_rows, double).astype(BF16)
        parts.append(jnp.concatenate([both[:, :width], both[:, width:]], axis=0))
    stores = []
    for r in range(rows):
        ordered = sum(reorder(pick_row.at[j], parts[j], r * feats, feats) for j in range(hl))
        cells_ref[r] = ordered.T.astype(BF16)
        stores.append(pltpu.make_async_copy(cells_ref.at[r], out_hbm.at[r], out_sems.at[r]))
        stores[-1].start()
    for j in range(hl):
        exchanged(send2, 1, 0, j)
    for store in stores:
        store.wait()


def body(sizes, cells, counts, train, gain, fi, fo, si, so, hu, hd):
    wide, narrow = sizes
    total = wide * narrow
    cells = jnp.swapaxes(cells, 1, 2)
    rows, width, feats = cells.shape
    hl = feats // total // 2
    pair = rows // 2
    half = rows * feats // 2
    all_rows = rows * total
    shard = fi.shape[0]
    anywhere = pl.BlockSpec(memory_space=pl.ANY)
    sems = pltpu.SemaphoreType.DMA((2, narrow))
    weight = pltpu.VMEM((narrow, 2, shard, 2 * width), BF16)
    first = pltpu.VMEM((2, total, pair * hl, 2 * width), BF16)
    last = pltpu.VMEM((hl, total, rows, 2 * width), BF16)
    out = pl.pallas_call(
        functools.partial(kernel, sizes),
        out_shape=jax.ShapeDtypeStruct(cells.shape, BF16),
        in_specs=[anywhere] * 10,
        out_specs=anywhere,
        scratch_shapes=[
            pltpu.SMEM(counts.shape, jnp.int32),
            pltpu.SMEM(train.shape, jnp.int32),
            pltpu.VMEM(gain.shape, F32),
            pltpu.VMEM(cells.shape, BF16),
            pltpu.VMEM((rows * feats, width), BF16),
            *[pltpu.VMEM(a.shape, BF16) for a in (fi, fo, si, so, hu, hd)],
            weight,
            weight,
            pltpu.VMEM((narrow, 4, shard, 2 * width), BF16),
            pltpu.VMEM((3, half, width), BF16),
            pltpu.VMEM((half, width), BF16),
            pltpu.VMEM((half, half), BF16),
            pltpu.VMEM((hl * all_rows, half), BF16),
            pltpu.VMEM((hl, rows * feats, half), BF16),
            pltpu.VMEM((HEADS * feats, width), BF16),
            pltpu.VMEM((HEADS * all_rows, width), BF16),
            first,
            first,
            last,
            last,
            pltpu.SemaphoreType.REGULAR,
            sems,
            sems,
            sems,
            sems,
            sems,
            sems,
            pltpu.SemaphoreType.DMA((2, narrow, wide // 2)),
            sems,
            sems,
            pltpu.SemaphoreType.DMA((2, 2, 2)),
            pltpu.SemaphoreType.DMA((10,)),
            pltpu.SemaphoreType.DMA((rows,)),
        ],
        compiler_params=pltpu.CompilerParams(
            collective_id=0, has_side_effects=True, vmem_limit_bytes=56 << 20
        ),
    )(counts, train, gain, cells, fi, fo, si, so, hu, hd)
    return jnp.swapaxes(out, 1, 2)


def solution(mesh):
    sizes = (mesh.shape["wide"], mesh.shape["narrow"])
    return jax.shard_map(
        functools.partial(body, sizes),
        mesh=mesh,
        in_specs=(
            P(("groups", "wide", "narrow"), None, None),
            P(("groups", "wide", "narrow")),
            P("groups"),
            P(),
            P("narrow", None),
            P("narrow", None),
            P("narrow", None),
            P("narrow", None),
            P("narrow", None),
            P("narrow", None),
        ),
        out_specs=P(("groups", "wide", "narrow"), None, None),
        check_vma=False,
    )
```

```python
import functools
import math

import jax
import jax.numpy as jnp
from jax import lax
from jax.experimental import pallas as pl
from jax.experimental.pallas import tpu as pltpu
from jax.sharding import PartitionSpec as P

HEADS = 6
EPSILON = 1e-05
MESH = pl.DeviceIdType.MESH
F32 = jnp.float32
BF16 = jnp.bfloat16


def normalize(values, gain):
    average = jnp.mean(values, axis=-1, keepdims=True)
    centered = values - average
    spread = jnp.mean(centered * centered, axis=-1, keepdims=True)
    return centered * lax.rsqrt(spread + EPSILON) * gain


def matmul(a, b):
    return jnp.dot(a, b, preferred_element_type=F32)


def gathered(ref, part):
    parts, _, rows, columns = ref.shape
    if rows % 16 == 0:
        return ref[:, part].reshape(parts * rows, columns)
    pieces = [ref[i, part].astype(F32) for i in range(parts)]
    return jnp.concatenate(pieces, axis=0).astype(BF16)


def gathered_down(ref, width):
    pieces = []
    for owner in range(ref.shape[0]):
        for part in (2, 3):
            both = ref[owner, part].astype(F32)
            pieces += [both[:, :width], both[:, width:]]
    return jnp.concatenate(pieces, axis=0).astype(BF16)


def one_hot(count, depth, start, source):
    to = lax.broadcasted_iota(jnp.int32, (count, 1), 0) + start
    column = lax.broadcasted_iota(jnp.int32, (count, depth), 1)
    return jnp.where(column == source(to), 1.0, 0.0).astype(BF16)


def prepare(ref, source, chunk=512):
    count, depth = ref.shape
    chunk = min(chunk, count)
    for start in range(0, count, chunk):
        ref[start : start + chunk, :] = one_hot(chunk, depth, start, source)


def reorder(pick, x, start=0, count=None, chunk=512):
    count = pick.shape[0] if count is None else count
    chunk = min(chunk, count)
    pieces = [
        matmul(pick[at : at + chunk, :], x) for at in range(start, start + count, chunk)
    ]
    return pieces[0] if len(pieces) == 1 else jnp.concatenate(pieces, axis=0)


def attend(q, k, v, bias, ones):
    length, width = q.shape
    head_size = width // HEADS
    factor = math.log2(math.e) / math.sqrt(head_size)
    head_of = lax.broadcasted_iota(jnp.int32, (length, width), 1) // head_size
    zero = jnp.zeros_like(k)
    masks = [head_of == h for h in range(HEADS)]
    keys = jnp.concatenate([jnp.where(m, k, zero) for m in masks], axis=0)
    values = jnp.concatenate([jnp.where(m, v, zero) for m in masks], axis=0)
    scores = lax.dot_general(q, keys, (((1,), (1,)), ((), ())), preferred_element_type=F32)
    powers = []
    for h in range(HEADS):
        s = scores[:, h * length : (h + 1) * length] * factor + bias
        powers.append(jnp.exp2(s - jnp.max(s, axis=-1, keepdims=True)).astype(BF16))
    weight = jnp.concatenate(powers, axis=1)
    return (matmul(weight, values) / matmul(weight, ones)).astype(BF16)


def head_ones(ref, length):
    row = lax.broadcasted_iota(jnp.int32, ref.shape, 0) // length
    lane = lax.broadcasted_iota(jnp.int32, ref.shape, 1) // (ref.shape[1] // HEADS)
    ref[...] = jnp.where(row == lane, 1.0, 0.0).astype(BF16)


def masks_of(length, width):
    head_of = lax.broadcasted_iota(jnp.int32, (length, width), 1) // (width // HEADS)
    return [head_of == h for h in range(HEADS)]


def stacked(v, masks):
    zero = jnp.zeros_like(v)
    return jnp.concatenate([jnp.where(m, v, zero) for m in masks], axis=0)


def attend_all(x, qk, v, length, bias_of, ones, hook):
    count, width = x.shape[0] // length, x.shape[1]
    factor = math.log2(math.e) / math.sqrt(width // HEADS)
    masks = masks_of(length, width)
    cuts = [slice(i * length, (i + 1) * length) for i in range(count)]
    scores = [
        lax.dot_general(
            qk[c, :width],
            stacked(qk[c, width:], masks),
            (((1,), (1,)), ((), ())),
            preferred_element_type=F32,
        )
        for c in cuts
    ]
    if hook is not None:
        hook()
    weights = []
    for i in range(count):
        powers = []
        for h in range(HEADS):
            s = scores[i][:, h * length : (h + 1) * length] + bias_of(i)
            powers.append(jnp.exp2((s - jnp.max(s, axis=-1, keepdims=True)) * factor).astype(BF16))
        weights.append(jnp.concatenate(powers, axis=1))
    done = [
        (matmul(p, stacked(v[c], masks)) / matmul(p, ones)).astype(BF16)
        for p, c in zip(weights, cuts)
    ]
    return jnp.concatenate(done, axis=0)


def attention_block(
    x, left, right, qkv_ref, ctx_ref, ones_ref, length, bias_of, gain, hook=None
):
    width = x.shape[1]
    qk = matmul(x, left).astype(BF16)
    v = matmul(x, right[:, :width]).astype(BF16)
    if length <= 128:
        ctx = attend_all(x, qk, v, length, bias_of, ones_ref[...], hook)
    else:
        if hook is not None:
            hook()
        qkv_ref[0] = qk[:, :width]
        qkv_ref[1] = qk[:, width:]
        qkv_ref[2] = v

        @pl.loop(0, x.shape[0] // length)
        def _(i):
            rows = pl.ds(pl.multiple_of(i * length, length), length)
            ctx_ref[rows, :] = attend(
                qkv_ref[0, rows, :],
                qkv_ref[1, rows, :],
                qkv_ref[2, rows, :],
                bias_of(i),
                ones_ref[...],
            )

        ctx = ctx_ref[...]
    update = matmul(ctx, right[:, width:])
    return normalize(x.astype(F32) + update, gain).astype(BF16)


def kernel(
    sizes,
    counts_hbm,
    train_hbm,
    gain_hbm,
    cells_hbm,
    fi_hbm,
    fo_hbm,
    si_hbm,
    so_hbm,
    hu_hbm,
    hd_hbm,
    out_hbm,
    counts_ref,
    train_ref,
    gain_ref,
    cells_ref,
    x_ref,
    fi_ref,
    fo_ref,
    si_ref,
    so_ref,
    hu_ref,
    hd_ref,
    wf,
    ws,
    wb,
    qkv,
    ctx,
    pick_send,
    pick_column,
    pick_row,
    feature_ones,
    sample_ones,
    send1,
    recv1,
    send2,
    recv2,
    ready,
    sa,
    ra,
    sb,
    rb,
    sz,
    rz,
    sp,
    sm,
    rm,
    cell_sems,
    load_sems,
    out_sems,
):
    wide, narrow = sizes
    total = wide * narrow
    chips = wide // 2
    g = lax.axis_index("groups")
    w = lax.axis_index("wide")
    n = lax.axis_index("narrow")
    me = w * narrow + n
    core = lax.rem(w, 2)
    chip = w // 2
    mate = w + 1 - 2 * core
    rows, width, feats = cells_ref.shape
    local = feats // total
    hl = local // 2
    pair = rows // 2
    piece = pair * hl
    all_rows = rows * total
    half_cells = rows * feats // 2

    barrier = pltpu.get_barrier_semaphore()
    for step in range(1, narrow):
        pl.semaphore_signal(
            barrier, inc=1, device_id=(g, w, lax.rem(n + step, narrow)), device_id_type=MESH
        )
    for step in range(1, wide):
        pl.semaphore_signal(
            barrier, inc=1, device_id=(g, lax.rem(w + step, wide), n), device_id_type=MESH
        )

    loads = [
        pltpu.make_async_copy(src, dst, load_sems.at[i])
        for i, (src, dst) in enumerate(
            (
                (fi_hbm, fi_ref),
                (fo_hbm, fo_ref),
                (cells_hbm, cells_ref),
                (si_hbm, si_ref),
                (so_hbm, so_ref),
                (hu_hbm, hu_ref),
                (hd_hbm, hd_ref),
                (gain_hbm, gain_ref),
                (counts_hbm, counts_ref),
                (train_hbm, train_ref),
            )
        )
    ]
    for load in loads:
        load.start()
    double = 2 * width
    shard = fi_ref.shape[0]
    loads[0].wait()
    loads[1].wait()
    wf[n, 0] = fi_ref[:, :double]
    wf[n, 1] = jnp.concatenate([fi_ref[:, double:], fo_ref[...]], axis=1)
    pl.semaphore_wait(barrier, narrow - 1 + wide - 1)

    weights = (wf, ws)
    steps = range(1, narrow)

    def along(group, step):
        ref = weights[group]
        return pltpu.make_async_remote_copy(
            src_ref=ref.at[n, core],
            dst_ref=ref.at[n, core],
            send_sem=sa.at[group, step],
            recv_sem=ra.at[group, step],
            device_id=(g, w, lax.rem(n + step, narrow)),
            device_id_type=MESH,
        )

    def across(group, step):
        ref = weights[group]
        owner = lax.rem(n - step + narrow, narrow)
        return pltpu.make_async_remote_copy(
            src_ref=ref.at[owner, core],
            dst_ref=ref.at[owner, core],
            send_sem=sb.at[group, step],
            recv_sem=rb.at[group, step],
            device_id=(g, mate, n),
            device_id_type=MESH,
        )

    def big(slot, step):
        block = core + 2 * slot
        return pltpu.make_async_remote_copy(
            src_ref=wb.at[n, block],
            dst_ref=wb.at[n, block],
            send_sem=sz.at[slot, step],
            recv_sem=rz.at[slot, step],
            device_id=(g, w, lax.rem(n + step, narrow)),
            device_id_type=MESH,
        )

    def spread(slot, step, to):
        block = core + 2 * slot
        owner = lax.rem(n - step + narrow, narrow)
        return pltpu.make_async_remote_copy(
            src_ref=wb.at[owner, block],
            dst_ref=wb.at[owner, block],
            send_sem=sp.at[slot, step, to],
            recv_sem=rz.at[slot, step],
            device_id=(g, lax.rem(w + 2 * to, wide), n),
            device_id_type=MESH,
        )

    def shared(slot, step):
        block = core + 2 * slot
        owner = lax.rem(n - step + narrow, narrow)
        return pltpu.make_async_remote_copy(
            src_ref=wb.at[owner, block],
            dst_ref=wb.at[owner, block],
            send_sem=sm.at[slot, step],
            recv_sem=rm.at[slot, step],
            device_id=(g, mate, n),
            device_id_type=MESH,
        )

    for step in steps:
        along(0, step).start()
    for step in steps:
        pl.semaphore_signal(
            ready, inc=1, device_id=(g, w, lax.rem(n + step, narrow)), device_id_type=MESH
        )

    for load in loads[3:7]:
        load.wait()
    ws[n, 0] = si_ref[:, :double]
    ws[n, 1] = jnp.concatenate([si_ref[:, double:], so_ref[...]], axis=1)
    wb[n, 0] = hu_ref[:, :double]
    wb[n, 1] = hu_ref[:, double:]
    down = hd_ref[...].astype(F32)
    for i in range(2):
        top = down[2 * i * shard : (2 * i + 1) * shard]
        low = down[(2 * i + 1) * shard : (2 * i + 2) * shard]
        wb[n, 2 + i] = jnp.concatenate([top, low], axis=1).astype(BF16)
    for slot in range(2):
        @pl.when(chip == core + 2 * slot)
        def _(slot=slot):
            for step in steps:
                big(slot, step).start()
    loads[2].wait()
    for r in range(rows):
        x_ref[r * feats : (r + 1) * feats, :] = cells_ref[r].astype(F32).T.astype(BF16)

    def to_send(i):
        h, k = i // (half_cells // 2), i % (half_cells // 2)
        d, r, j = k // piece, (k % piece) // hl, k % hl
        return r * feats + d * local + h * hl + j

    def to_column(i):
        j, k = i // all_rows, i % all_rows
        s, r = k // rows, k % rows
        return (r // pair) * (total * piece) + s * piece + (r % pair) * hl + j

    def to_row(j):
        def source(i):
            r, f = i // feats, i % feats
            d, h, at = f // local, (f % local) // hl, f % hl
            k = h * all_rows + d * rows + r
            return jnp.where(at == j, k, -1)

        return source

    prepare(pick_send, to_send)
    prepare(pick_column, to_column)
    for j in range(hl):
        prepare(pick_row.at[j], to_row(j))
    head_ones(feature_ones, feats)
    head_ones(sample_ones, all_rows)
    for load in loads[7:]:
        load.wait()

    for step in steps:
        along(0, step).wait_recv()
        across(0, step).start()
    for step in steps:
        along(1, step).start()
    for step in steps:
        across(0, step).wait_recv()

    near = [(a, b) for b in range(narrow) for a in range(wide) if a or b]
    near.sort(key=lambda t: (-min(t[1], narrow - t[1]), -min(t[0], wide - t[0])))

    def copy_to(send, recv, index, part, a, b):
        tw, tn = lax.rem(w + a, wide), lax.rem(n + b, narrow)
        return pltpu.make_async_remote_copy(
            src_ref=send.at[part, tw * narrow + tn],
            dst_ref=recv.at[part, me],
            send_sem=cell_sems.at[index, 0, part],
            recv_sem=cell_sems.at[index, 1, part],
            device_id=(g, tw, tn),
            device_id_type=MESH,
        )

    def exchange(send, recv, index, part):
        recv[part, me] = send[part, me]
        if total <= 32:
            for a, b in near:
                copy_to(send, recv, index, part, a, b).start()
        else:
            @pl.loop(1, total)
            def _(step):
                copy_to(send, recv, index, part, step // narrow, lax.rem(step, narrow)).start()

    def exchanged(ref, index, way, part):
        whole = ref.at[part, pl.ds(0, total - 1)]
        pltpu.make_async_copy(whole, whole, cell_sems.at[index, way, part]).wait()

    keys = lax.broadcasted_iota(jnp.int32, (1, feats), 1)
    left, right = gathered(wf, 0), gathered(wf, 1)
    def relay():
        for slot in range(2):
            @pl.when(chip == core + 2 * slot)
            def _(slot=slot):
                for step in steps:
                    big(slot, step).wait_recv()
                    for to in range(1, chips):
                        spread(slot, step, to).start()
                    shared(slot, step).start()

    for q in range(2):
        x = x_ref[q * half_cells : (q + 1) * half_cells, :]
        first = attention_block(
            x,
            left,
            right,
            qkv,
            ctx,
            feature_ones,
            feats,
            lambda i: jnp.where(keys < counts_ref[q * pair + i], 0.0, -1e30),
            gain_ref[0:1, :],
            None,
        )
        picked = reorder(pick_send, first)
        both = jnp.concatenate([picked[: half_cells // 2], picked[half_cells // 2 :]], axis=1)
        send1[q] = both.reshape(total, piece, double).astype(BF16)
        if q == 0:
            pl.semaphore_wait(ready, narrow - 1)
        exchange(send1, recv1, 0, q)
        if q == 0:
            relay()

    for step in steps:
        along(1, step).wait_recv()
        across(1, step).start()
    for slot in range(2):
        @pl.when(chip != core + 2 * slot)
        def _(slot=slot):
            for step in steps:
                big(slot, step).wait_recv()
                shared(slot, step).start()
    for step in steps:
        across(1, step).wait_recv()
    left, right = gathered(ws, 0), gathered(ws, 1)
    for q in range(2):
        exchanged(recv1, 0, 1, q)

    samples = lax.broadcasted_iota(jnp.int32, (1, all_rows), 1)
    sample_bias = jnp.where(samples < train_ref[0], 0.0, -1e30)
    landed = jnp.concatenate(
        [recv1[q].astype(F32).reshape(total * piece, double).astype(BF16) for q in range(2)], axis=0
    )
    tile = min(512, half_cells)
    for j in range(hl):
        y = reorder(pick_column, landed, j * all_rows, all_rows).astype(BF16)
        y = jnp.concatenate([y[:, :width], y[:, width:]], axis=0)
        second = attention_block(
            y, left, right, qkv, ctx, sample_ones, all_rows, lambda i: sample_bias, gain_ref[1:2, :]
        )
        ctx[...] = second
        if j == 0:
            for step in steps:
                for slot in range(2):
                    shared(slot, step).wait_recv()
            up = [gathered(wb, c) for c in range(2)]
            low = gathered_down(wb, width)

        def feed(i):
            at = pl.ds(pl.multiple_of(i * tile, tile), tile)
            values = ctx[at, :]
            halves = []
            for c in range(2):
                h = matmul(values, up[c])
                halves.append((0.5 * h * (1.0 + lax.erf(h * (2.0**-0.5)))).astype(BF16))
            back = matmul(jnp.concatenate(halves, axis=1), low)
            ctx[at, :] = normalize(values.astype(F32) + back, gain_ref[2:3, :]).astype(BF16)

        if half_cells == tile:
            feed(0)
        else:
            pl.loop(0, half_cells // tile)(feed)
        done = jnp.concatenate([ctx[:all_rows, :], ctx[all_rows:, :]], axis=1)
        send2[j] = done.astype(F32).reshape(total, rows, double).astype(BF16)
        exchange(send2, recv2, 1, j)

    for step in steps:
        for group in range(2):
            along(group, step).wait_send()
            across(group, step).wait_send()
        for slot in range(2):
            @pl.when(chip == core + 2 * slot)
            def _(slot=slot, step=step):
                big(slot, step).wait_send()
                for to in range(1, chips):
                    spread(slot, step, to).wait_send()

            shared(slot, step).wait_send()
    for q in range(2):
        exchanged(send1, 0, 0, q)

    parts = []
    for j in range(hl):
        exchanged(recv2, 1, 1, j)
        both = recv2[j].astype(F32).reshape(all_rows, double).astype(BF16)
        parts.append(jnp.concatenate([both[:, :width], both[:, width:]], axis=0))
    for r in range(rows):
        ordered = sum(reorder(pick_row.at[j], parts[j], r * feats, feats) for j in range(hl))
        out_hbm[r] = ordered.T.astype(BF16)
    for j in range(hl):
        exchanged(send2, 1, 0, j)


def body(sizes, cells, counts, train, gain, fi, fo, si, so, hu, hd):
    wide, narrow = sizes
    total = wide * narrow
    cells = jnp.swapaxes(cells, 1, 2)
    rows, width, feats = cells.shape
    hl = feats // total // 2
    pair = rows // 2
    half = rows * feats // 2
    all_rows = rows * total
    shard = fi.shape[0]
    anywhere = pl.BlockSpec(memory_space=pl.ANY)
    sems = pltpu.SemaphoreType.DMA((2, narrow))
    weight = pltpu.VMEM((narrow, 2, shard, 2 * width), BF16)
    first = pltpu.VMEM((2, total, pair * hl, 2 * width), BF16)
    last = pltpu.VMEM((hl, total, rows, 2 * width), BF16)
    out = pl.pallas_call(
        functools.partial(kernel, sizes),
        out_shape=pltpu.VMEM(cells.shape, BF16),
        in_specs=[pl.BlockSpec(memory_space=pltpu.HBM)] * 10,
        out_specs=pl.BlockSpec(memory_space=pltpu.VMEM),
        scratch_shapes=[
            pltpu.SMEM(counts.shape, jnp.int32),
            pltpu.SMEM(train.shape, jnp.int32),
            pltpu.VMEM(gain.shape, F32),
            pltpu.VMEM(cells.shape, BF16),
            pltpu.VMEM((rows * feats, width), BF16),
            *[pltpu.VMEM(a.shape, BF16) for a in (fi, fo, si, so, hu, hd)],
            weight,
            weight,
            pltpu.VMEM((narrow, 4, shard, 2 * width), BF16),
            pltpu.VMEM((3, half, width), BF16),
            pltpu.VMEM((half, width), BF16),
            pltpu.VMEM((half, half), BF16),
            pltpu.VMEM((hl * all_rows, half), BF16),
            pltpu.VMEM((hl, rows * feats, half), BF16),
            pltpu.VMEM((HEADS * feats, width), BF16),
            pltpu.VMEM((HEADS * all_rows, width), BF16),
            first,
            first,
            last,
            last,
            pltpu.SemaphoreType.REGULAR,
            sems,
            sems,
            sems,
            sems,
            sems,
            sems,
            pltpu.SemaphoreType.DMA((2, narrow, wide // 2)),
            sems,
            sems,
            pltpu.SemaphoreType.DMA((2, 2, 2)),
            pltpu.SemaphoreType.DMA((10,)),
            pltpu.SemaphoreType.DMA((rows,)),
        ],
        compiler_params=pltpu.CompilerParams(
            collective_id=0, has_side_effects=True, vmem_limit_bytes=56 << 20
        ),
    )(counts, train, gain, cells, fi, fo, si, so, hu, hd)
    return jnp.swapaxes(out, 1, 2)


def solution(mesh):
    sizes = (mesh.shape["wide"], mesh.shape["narrow"])
    return jax.shard_map(
        functools.partial(body, sizes),
        mesh=mesh,
        in_specs=(
            P(("groups", "wide", "narrow"), None, None),
            P(("groups", "wide", "narrow")),
            P("groups"),
            P(),
            P("narrow", None),
            P("narrow", None),
            P("narrow", None),
            P("narrow", None),
            P("narrow", None),
            P("narrow", None),
        ),
        out_specs=P(("groups", "wide", "narrow"), None, None),
        check_vma=False,
    )
```

```python
import functools
import math

import jax
import jax.numpy as jnp
from jax import lax
from jax.experimental import pallas as pl
from jax.experimental.pallas import tpu as pltpu
from jax.sharding import PartitionSpec as P

HEADS = 6
EPSILON = 1e-05
MESH = pl.DeviceIdType.MESH
F32 = jnp.float32
BF16 = jnp.bfloat16


def normalize(values, gain):
    average = jnp.mean(values, axis=-1, keepdims=True)
    centered = values - average
    spread = jnp.mean(centered * centered, axis=-1, keepdims=True)
    return centered * lax.rsqrt(spread + EPSILON) * gain


def matmul(a, b):
    return jnp.dot(a, b, preferred_element_type=F32)


def gathered(ref, part):
    parts, _, rows, columns = ref.shape
    if rows % 16 == 0:
        return ref[:, part].reshape(parts * rows, columns)
    pieces = [ref[i, part].astype(F32) for i in range(parts)]
    return jnp.concatenate(pieces, axis=0).astype(BF16)


def gathered_down(ref, width):
    pieces = []
    for owner in range(ref.shape[0]):
        for part in (2, 3):
            both = ref[owner, part].astype(F32)
            pieces += [both[:, :width], both[:, width:]]
    return jnp.concatenate(pieces, axis=0).astype(BF16)


def one_hot(count, depth, start, source):
    to = lax.broadcasted_iota(jnp.int32, (count, 1), 0) + start
    column = lax.broadcasted_iota(jnp.int32, (count, depth), 1)
    return jnp.where(column == source(to), 1.0, 0.0).astype(BF16)


def prepare(ref, source, chunk=512):
    count, depth = ref.shape
    chunk = min(chunk, count)
    for start in range(0, count, chunk):
        ref[start : start + chunk, :] = one_hot(chunk, depth, start, source)


def reorder(pick, x, start=0, count=None, chunk=512):
    count = pick.shape[0] if count is None else count
    chunk = min(chunk, count)
    pieces = [
        matmul(pick[at : at + chunk, :], x) for at in range(start, start + count, chunk)
    ]
    return pieces[0] if len(pieces) == 1 else jnp.concatenate(pieces, axis=0)


def attend(q, k, v, bias, ones):
    length, width = q.shape
    head_size = width // HEADS
    factor = math.log2(math.e) / math.sqrt(head_size)
    head_of = lax.broadcasted_iota(jnp.int32, (length, width), 1) // head_size
    zero = jnp.zeros_like(k)
    masks = [head_of == h for h in range(HEADS)]
    keys = jnp.concatenate([jnp.where(m, k, zero) for m in masks], axis=0)
    values = jnp.concatenate([jnp.where(m, v, zero) for m in masks], axis=0)
    scores = lax.dot_general(q, keys, (((1,), (1,)), ((), ())), preferred_element_type=F32)
    powers = []
    for h in range(HEADS):
        s = scores[:, h * length : (h + 1) * length] * factor + bias
        powers.append(jnp.exp2(s - jnp.max(s, axis=-1, keepdims=True)).astype(BF16))
    weight = jnp.concatenate(powers, axis=1)
    return (matmul(weight, values) / matmul(weight, ones)).astype(BF16)


def head_ones(ref, length):
    row = lax.broadcasted_iota(jnp.int32, ref.shape, 0) // length
    lane = lax.broadcasted_iota(jnp.int32, ref.shape, 1) // (ref.shape[1] // HEADS)
    ref[...] = jnp.where(row == lane, 1.0, 0.0).astype(BF16)


def masks_of(length, width):
    head_of = lax.broadcasted_iota(jnp.int32, (length, width), 1) // (width // HEADS)
    return [head_of == h for h in range(HEADS)]


def stacked(v, masks):
    zero = jnp.zeros_like(v)
    return jnp.concatenate([jnp.where(m, v, zero) for m in masks], axis=0)


def attend_all(x, qk, v, length, bias_of, ones, hook):
    count, width = x.shape[0] // length, x.shape[1]
    factor = math.log2(math.e) / math.sqrt(width // HEADS)
    masks = masks_of(length, width)
    cuts = [slice(i * length, (i + 1) * length) for i in range(count)]
    scores = [
        lax.dot_general(
            qk[c, :width],
            stacked(qk[c, width:], masks),
            (((1,), (1,)), ((), ())),
            preferred_element_type=F32,
        )
        for c in cuts
    ]
    if hook is not None:
        hook()
    weights = []
    for i in range(count):
        powers = []
        for h in range(HEADS):
            s = scores[i][:, h * length : (h + 1) * length] + bias_of(i)
            powers.append(jnp.exp2((s - jnp.max(s, axis=-1, keepdims=True)) * factor).astype(BF16))
        weights.append(jnp.concatenate(powers, axis=1))
    done = [
        (matmul(p, stacked(v[c], masks)) / matmul(p, ones)).astype(BF16)
        for p, c in zip(weights, cuts)
    ]
    return jnp.concatenate(done, axis=0)


def attention_block(
    x, left, right, qkv_ref, ctx_ref, ones_ref, length, bias_of, gain, hook=None
):
    width = x.shape[1]
    qk = matmul(x, left).astype(BF16)
    v = matmul(x, right[:, :width]).astype(BF16)
    if length <= 128:
        ctx = attend_all(x, qk, v, length, bias_of, ones_ref[...], hook)
    else:
        if hook is not None:
            hook()
        qkv_ref[0] = qk[:, :width]
        qkv_ref[1] = qk[:, width:]
        qkv_ref[2] = v

        @pl.loop(0, x.shape[0] // length)
        def _(i):
            rows = pl.ds(pl.multiple_of(i * length, length), length)
            ctx_ref[rows, :] = attend(
                qkv_ref[0, rows, :],
                qkv_ref[1, rows, :],
                qkv_ref[2, rows, :],
                bias_of(i),
                ones_ref[...],
            )

        ctx = ctx_ref[...]
    update = matmul(ctx, right[:, width:])
    return normalize(x.astype(F32) + update, gain).astype(BF16)


def kernel(
    sizes,
    counts_hbm,
    train_hbm,
    gain_hbm,
    cells_hbm,
    fi_hbm,
    fo_hbm,
    si_hbm,
    so_hbm,
    hu_hbm,
    hd_hbm,
    out_hbm,
    counts_ref,
    train_ref,
    gain_ref,
    cells_ref,
    x_ref,
    fi_ref,
    fo_ref,
    si_ref,
    so_ref,
    hu_ref,
    hd_ref,
    wf,
    ws,
    wb,
    qkv,
    ctx,
    pick_send,
    pick_column,
    pick_row,
    feature_ones,
    sample_ones,
    send1,
    recv1,
    send2,
    recv2,
    ready,
    sa,
    ra,
    sb,
    rb,
    sz,
    rz,
    sp,
    sm,
    rm,
    cell_sems,
    load_sems,
    out_sems,
):
    wide, narrow = sizes
    total = wide * narrow
    chips = wide // 2
    g = lax.axis_index("groups")
    w = lax.axis_index("wide")
    n = lax.axis_index("narrow")
    me = w * narrow + n
    core = lax.rem(w, 2)
    chip = w // 2
    mate = w + 1 - 2 * core
    rows, width, feats = cells_ref.shape
    local = feats // total
    hl = local // 2
    pair = rows // 2
    piece = pair * hl
    all_rows = rows * total
    half_cells = rows * feats // 2

    barrier = pltpu.get_barrier_semaphore()
    for step in range(1, narrow):
        pl.semaphore_signal(
            barrier, inc=1, device_id=(g, w, lax.rem(n + step, narrow)), device_id_type=MESH
        )
    for step in range(1, wide):
        pl.semaphore_signal(
            barrier, inc=1, device_id=(g, lax.rem(w + step, wide), n), device_id_type=MESH
        )

    loads = [
        pltpu.make_async_copy(src, dst, load_sems.at[i])
        for i, (src, dst) in enumerate(
            (
                (fi_hbm, fi_ref),
                (fo_hbm, fo_ref),
                (cells_hbm, cells_ref),
                (si_hbm, si_ref),
                (so_hbm, so_ref),
                (hu_hbm, hu_ref),
                (hd_hbm, hd_ref),
                (gain_hbm, gain_ref),
                (counts_hbm, counts_ref),
                (train_hbm, train_ref),
            )
        )
    ]
    for load in loads:
        load.start()
    double = 2 * width
    shard = fi_ref.shape[0]
    loads[0].wait()
    loads[1].wait()
    wf[n, 0] = fi_ref[:, :double]
    wf[n, 1] = jnp.concatenate([fi_ref[:, double:], fo_ref[...]], axis=1)
    pl.semaphore_wait(barrier, narrow - 1 + wide - 1)

    weights = (wf, ws)
    steps = range(1, narrow)

    def along(group, step):
        ref = weights[group]
        return pltpu.make_async_remote_copy(
            src_ref=ref.at[n, core],
            dst_ref=ref.at[n, core],
            send_sem=sa.at[group, step],
            recv_sem=ra.at[group, step],
            device_id=(g, w, lax.rem(n + step, narrow)),
            device_id_type=MESH,
        )

    def across(group, step):
        ref = weights[group]
        owner = lax.rem(n - step + narrow, narrow)
        return pltpu.make_async_remote_copy(
            src_ref=ref.at[owner, core],
            dst_ref=ref.at[owner, core],
            send_sem=sb.at[group, step],
            recv_sem=rb.at[group, step],
            device_id=(g, mate, n),
            device_id_type=MESH,
        )

    def big(slot, step):
        block = core + 2 * slot
        return pltpu.make_async_remote_copy(
            src_ref=wb.at[n, block],
            dst_ref=wb.at[n, block],
            send_sem=sz.at[slot, step],
            recv_sem=rz.at[slot, step],
            device_id=(g, w, lax.rem(n + step, narrow)),
            device_id_type=MESH,
        )

    def spread(slot, step, to):
        block = core + 2 * slot
        owner = lax.rem(n - step + narrow, narrow)
        return pltpu.make_async_remote_copy(
            src_ref=wb.at[owner, block],
            dst_ref=wb.at[owner, block],
            send_sem=sp.at[slot, step, to],
            recv_sem=rz.at[slot, step],
            device_id=(g, lax.rem(w + 2 * to, wide), n),
            device_id_type=MESH,
        )

    def shared(slot, step):
        block = core + 2 * slot
        owner = lax.rem(n - step + narrow, narrow)
        return pltpu.make_async_remote_copy(
            src_ref=wb.at[owner, block],
            dst_ref=wb.at[owner, block],
            send_sem=sm.at[slot, step],
            recv_sem=rm.at[slot, step],
            device_id=(g, mate, n),
            device_id_type=MESH,
        )

    for step in steps:
        along(0, step).start()
    for step in steps:
        pl.semaphore_signal(
            ready, inc=1, device_id=(g, w, lax.rem(n + step, narrow)), device_id_type=MESH
        )

    for load in loads[3:7]:
        load.wait()
    ws[n, 0] = si_ref[:, :double]
    ws[n, 1] = jnp.concatenate([si_ref[:, double:], so_ref[...]], axis=1)
    wb[n, 0] = hu_ref[:, :double]
    wb[n, 1] = hu_ref[:, double:]
    down = hd_ref[...].astype(F32)
    for i in range(2):
        top = down[2 * i * shard : (2 * i + 1) * shard]
        low = down[(2 * i + 1) * shard : (2 * i + 2) * shard]
        wb[n, 2 + i] = jnp.concatenate([top, low], axis=1).astype(BF16)
    loads[2].wait()
    for r in range(rows):
        x_ref[r * feats : (r + 1) * feats, :] = cells_ref[r].astype(F32).T.astype(BF16)

    def to_send(i):
        h, k = i // (half_cells // 2), i % (half_cells // 2)
        d, r, j = k // piece, (k % piece) // hl, k % hl
        return r * feats + d * local + h * hl + j

    def to_column(i):
        j, k = i // all_rows, i % all_rows
        s, r = k // rows, k % rows
        return (r // pair) * (total * piece) + s * piece + (r % pair) * hl + j

    def to_row(j):
        def source(i):
            r, f = i // feats, i % feats
            d, h, at = f // local, (f % local) // hl, f % hl
            k = h * all_rows + d * rows + r
            return jnp.where(at == j, k, -1)

        return source

    prepare(pick_send, to_send)
    prepare(pick_column, to_column)
    for j in range(hl):
        prepare(pick_row.at[j], to_row(j))
    head_ones(feature_ones, feats)
    head_ones(sample_ones, all_rows)
    for load in loads[7:]:
        load.wait()

    for step in steps:
        along(0, step).wait_recv()
        across(0, step).start()
    for step in steps:
        along(1, step).start()
    for step in steps:
        across(0, step).wait_recv()

    def flipped(value, bits):
        at = 1
        for _ in range(bits.bit_length()):
            if bits & at:
                value = value + at * (1 - 2 * lax.rem(value // at, 2))
            at *= 2
        return value

    def copy_to(send, recv, index, part, tw, tn):
        return pltpu.make_async_remote_copy(
            src_ref=send.at[part, tw * narrow + tn],
            dst_ref=recv.at[part, me],
            send_sem=cell_sems.at[index, 0, part],
            recv_sem=cell_sems.at[index, 1, part],
            device_id=(g, tw, tn),
            device_id_type=MESH,
        )

    others = [
        (flipped(w, a), flipped(n, b))
        for b in reversed(range(narrow))
        for a in reversed(range(wide))
        if total <= 32 and (a or b)
    ]

    def exchange(send, recv, index, part):
        recv[part, me] = send[part, me]
        if total <= 32:
            for tw, tn in others:
                copy_to(send, recv, index, part, tw, tn).start()
        else:
            @pl.loop(1, total)
            def _(step):
                to = lax.rem(me + step, total)
                copy_to(send, recv, index, part, to // narrow, lax.rem(to, narrow)).start()

    def exchanged(ref, index, way, part):
        whole = ref.at[part, pl.ds(0, total - 1)]
        pltpu.make_async_copy(whole, whole, cell_sems.at[index, way, part]).wait()

    keys = lax.broadcasted_iota(jnp.int32, (1, feats), 1)
    left, right = gathered(wf, 0), gathered(wf, 1)
    for q in range(2):
        x = x_ref[q * half_cells : (q + 1) * half_cells, :]
        first = attention_block(
            x,
            left,
            right,
            qkv,
            ctx,
            feature_ones,
            feats,
            lambda i: jnp.where(keys < counts_ref[q * pair + i], 0.0, -1e30),
            gain_ref[0:1, :],
            None,
        )
        picked = reorder(pick_send, first)
        both = jnp.concatenate([picked[: half_cells // 2], picked[half_cells // 2 :]], axis=1)
        send1[q] = both.reshape(total, piece, double).astype(BF16)
        if q == 0:
            pl.semaphore_wait(ready, narrow - 1)
        exchange(send1, recv1, 0, q)

    for slot in range(2):
        @pl.when(chip == core + 2 * slot)
        def _(slot=slot):
            for step in steps:
                big(slot, step).start()
    for step in steps:
        along(1, step).wait_recv()
        across(1, step).start()
    for step in steps:
        across(1, step).wait_recv()
    left, right = gathered(ws, 0), gathered(ws, 1)
    for q in range(2):
        exchanged(recv1, 0, 1, q)
    for slot in range(2):
        @pl.when(chip == core + 2 * slot)
        def _(slot=slot):
            for step in steps:
                big(slot, step).wait_recv()
                for to in range(1, chips):
                    spread(slot, step, to).start()
                shared(slot, step).start()

    samples = lax.broadcasted_iota(jnp.int32, (1, all_rows), 1)
    sample_bias = jnp.where(samples < train_ref[0], 0.0, -1e30)
    landed = jnp.concatenate(
        [recv1[q].astype(F32).reshape(total * piece, double).astype(BF16) for q in range(2)], axis=0
    )
    for j in range(hl):
        y = reorder(pick_column, landed, j * all_rows, all_rows).astype(BF16)
        y = jnp.concatenate([y[:, :width], y[:, width:]], axis=0)
        second = attention_block(
            y, left, right, qkv, ctx, sample_ones, all_rows, lambda i: sample_bias, gain_ref[1:2, :]
        )
        done = jnp.concatenate([second[:all_rows, :], second[all_rows:, :]], axis=1)
        send2[j] = done.astype(F32).reshape(total, rows, double).astype(BF16)
        exchange(send2, recv2, 1, j)

    for slot in range(2):
        @pl.when(chip != core + 2 * slot)
        def _(slot=slot):
            for step in steps:
                big(slot, step).wait_recv()
                shared(slot, step).start()

    for step in steps:
        for group in range(2):
            along(group, step).wait_send()
            across(group, step).wait_send()
        for slot in range(2):
            @pl.when(chip == core + 2 * slot)
            def _(slot=slot, step=step):
                big(slot, step).wait_send()
                for to in range(1, chips):
                    spread(slot, step, to).wait_send()

            shared(slot, step).wait_send()
    for q in range(2):
        exchanged(send1, 0, 0, q)

    tile = min(512, half_cells)
    parts = []
    for step in steps:
        for slot in range(2):
            shared(slot, step).wait_recv()
    up = [gathered(wb, c) for c in range(2)]
    low = gathered_down(wb, width)

    def feed(values):
        halves = []
        for c in range(2):
            h = matmul(values, up[c])
            halves.append((0.5 * h * (1.0 + lax.erf(h * (2.0**-0.5)))).astype(BF16))
        back = matmul(jnp.concatenate(halves, axis=1), low)
        return normalize(values.astype(F32) + back, gain_ref[2:3, :]).astype(BF16)

    for j in range(hl):
        exchanged(recv2, 1, 1, j)
        both = recv2[j].astype(F32).reshape(all_rows, double).astype(BF16)
        values = jnp.concatenate([both[:, :width], both[:, width:]], axis=0)
        if half_cells == tile:
            parts.append(feed(values))
            continue
        ctx[...] = values

        @pl.loop(0, half_cells // tile)
        def _(i):
            at = pl.ds(pl.multiple_of(i * tile, tile), tile)
            ctx[at, :] = feed(ctx[at, :])

        parts.append(ctx[...])
    for r in range(rows):
        ordered = sum(reorder(pick_row.at[j], parts[j], r * feats, feats) for j in range(hl))
        out_hbm[r] = ordered.T.astype(BF16)
    for j in range(hl):
        exchanged(send2, 1, 0, j)


def body(sizes, cells, counts, train, gain, fi, fo, si, so, hu, hd):
    wide, narrow = sizes
    total = wide * narrow
    cells = jnp.swapaxes(cells, 1, 2)
    rows, width, feats = cells.shape
    hl = feats // total // 2
    pair = rows // 2
    half = rows * feats // 2
    all_rows = rows * total
    shard = fi.shape[0]
    anywhere = pl.BlockSpec(memory_space=pl.ANY)
    sems = pltpu.SemaphoreType.DMA((2, narrow))
    weight = pltpu.VMEM((narrow, 2, shard, 2 * width), BF16)
    first = pltpu.VMEM((2, total, pair * hl, 2 * width), BF16)
    last = pltpu.VMEM((hl, total, rows, 2 * width), BF16)
    out = pl.pallas_call(
        functools.partial(kernel, sizes),
        out_shape=pltpu.VMEM(cells.shape, BF16),
        in_specs=[pl.BlockSpec(memory_space=pltpu.HBM)] * 10,
        out_specs=pl.BlockSpec(memory_space=pltpu.VMEM),
        scratch_shapes=[
            pltpu.SMEM(counts.shape, jnp.int32),
            pltpu.SMEM(train.shape, jnp.int32),
            pltpu.VMEM(gain.shape, F32),
            pltpu.VMEM(cells.shape, BF16),
            pltpu.VMEM((rows * feats, width), BF16),
            *[pltpu.VMEM(a.shape, BF16) for a in (fi, fo, si, so, hu, hd)],
            weight,
            weight,
            pltpu.VMEM((narrow, 4, shard, 2 * width), BF16),
            pltpu.VMEM((3, half, width), BF16),
            pltpu.VMEM((half, width), BF16),
            pltpu.VMEM((half, half), BF16),
            pltpu.VMEM((hl * all_rows, half), BF16),
            pltpu.VMEM((hl, rows * feats, half), BF16),
            pltpu.VMEM((HEADS * feats, width), BF16),
            pltpu.VMEM((HEADS * all_rows, width), BF16),
            first,
            first,
            last,
            last,
            pltpu.SemaphoreType.REGULAR,
            sems,
            sems,
            sems,
            sems,
            sems,
            sems,
            pltpu.SemaphoreType.DMA((2, narrow, wide // 2)),
            sems,
            sems,
            pltpu.SemaphoreType.DMA((2, 2, 2)),
            pltpu.SemaphoreType.DMA((10,)),
            pltpu.SemaphoreType.DMA((rows,)),
        ],
        compiler_params=pltpu.CompilerParams(
            collective_id=0, has_side_effects=True, vmem_limit_bytes=56 << 20
        ),
    )(counts, train, gain, cells, fi, fo, si, so, hu, hd)
    return jnp.swapaxes(out, 1, 2)


def solution(mesh):
    sizes = (mesh.shape["wide"], mesh.shape["narrow"])
    return jax.shard_map(
        functools.partial(body, sizes),
        mesh=mesh,
        in_specs=(
            P(("groups", "wide", "narrow"), None, None),
            P(("groups", "wide", "narrow")),
            P("groups"),
            P(),
            P("narrow", None),
            P("narrow", None),
            P("narrow", None),
            P("narrow", None),
            P("narrow", None),
            P("narrow", None),
        ),
        out_specs=P(("groups", "wide", "narrow"), None, None),
        check_vma=False,
    )
```

```python
import functools
import math

import jax
import jax.numpy as jnp
from jax import lax
from jax.experimental import pallas as pl
from jax.experimental.pallas import tpu as pltpu
from jax.sharding import PartitionSpec as P

HEADS = 6
EPSILON = 1e-05
MESH = pl.DeviceIdType.MESH
F32 = jnp.float32
BF16 = jnp.bfloat16


def normalize(values, gain):
    average = jnp.mean(values, axis=-1, keepdims=True)
    centered = values - average
    spread = jnp.mean(centered * centered, axis=-1, keepdims=True)
    return centered * lax.rsqrt(spread + EPSILON) * gain


def matmul(a, b):
    return jnp.dot(a, b, preferred_element_type=F32)


def gathered(ref, part):
    parts, _, rows, columns = ref.shape
    if rows % 16 == 0:
        return ref[:, part].reshape(parts * rows, columns)
    pieces = [ref[i, part].astype(F32) for i in range(parts)]
    return jnp.concatenate(pieces, axis=0).astype(BF16)


def gathered_down(ref, width):
    pieces = []
    for owner in range(ref.shape[0]):
        for part in (2, 3):
            both = ref[owner, part].astype(F32)
            pieces += [both[:, :width], both[:, width:]]
    return jnp.concatenate(pieces, axis=0).astype(BF16)


def one_hot(count, depth, start, source):
    to = lax.broadcasted_iota(jnp.int32, (count, 1), 0) + start
    column = lax.broadcasted_iota(jnp.int32, (count, depth), 1)
    return jnp.where(column == source(to), 1.0, 0.0).astype(BF16)


def prepare(ref, source, chunk=512):
    count, depth = ref.shape
    chunk = min(chunk, count)
    for start in range(0, count, chunk):
        ref[start : start + chunk, :] = one_hot(chunk, depth, start, source)


def reorder(pick, x, start=0, count=None, chunk=512):
    count = pick.shape[0] if count is None else count
    chunk = min(chunk, count)
    pieces = [
        matmul(pick[at : at + chunk, :], x) for at in range(start, start + count, chunk)
    ]
    return pieces[0] if len(pieces) == 1 else jnp.concatenate(pieces, axis=0)


def attend(q, k, v, bias, ones):
    length, width = q.shape
    head_size = width // HEADS
    factor = math.log2(math.e) / math.sqrt(head_size)
    head_of = lax.broadcasted_iota(jnp.int32, (length, width), 1) // head_size
    zero = jnp.zeros_like(k)
    masks = [head_of == h for h in range(HEADS)]
    keys = jnp.concatenate([jnp.where(m, k, zero) for m in masks], axis=0)
    values = jnp.concatenate([jnp.where(m, v, zero) for m in masks], axis=0)
    scores = lax.dot_general(q, keys, (((1,), (1,)), ((), ())), preferred_element_type=F32)
    powers = []
    for h in range(HEADS):
        s = scores[:, h * length : (h + 1) * length] * factor + bias
        powers.append(jnp.exp2(s - jnp.max(s, axis=-1, keepdims=True)).astype(BF16))
    weight = jnp.concatenate(powers, axis=1)
    return (matmul(weight, values) / matmul(weight, ones)).astype(BF16)


def head_ones(ref, length):
    row = lax.broadcasted_iota(jnp.int32, ref.shape, 0) // length
    lane = lax.broadcasted_iota(jnp.int32, ref.shape, 1) // (ref.shape[1] // HEADS)
    ref[...] = jnp.where(row == lane, 1.0, 0.0).astype(BF16)


def masks_of(length, width):
    head_of = lax.broadcasted_iota(jnp.int32, (length, width), 1) // (width // HEADS)
    return [head_of == h for h in range(HEADS)]


def stacked(v, masks):
    zero = jnp.zeros_like(v)
    return jnp.concatenate([jnp.where(m, v, zero) for m in masks], axis=0)


def attend_all(x, qk, v, length, bias_of, ones, hook):
    count, width = x.shape[0] // length, x.shape[1]
    factor = math.log2(math.e) / math.sqrt(width // HEADS)
    masks = masks_of(length, width)
    cuts = [slice(i * length, (i + 1) * length) for i in range(count)]
    scores = [
        lax.dot_general(
            qk[c, :width],
            stacked(qk[c, width:], masks),
            (((1,), (1,)), ((), ())),
            preferred_element_type=F32,
        )
        for c in cuts
    ]
    if hook is not None:
        hook()
    weights = []
    for i in range(count):
        powers = []
        for h in range(HEADS):
            s = scores[i][:, h * length : (h + 1) * length] + bias_of(i)
            powers.append(jnp.exp2((s - jnp.max(s, axis=-1, keepdims=True)) * factor).astype(BF16))
        weights.append(jnp.concatenate(powers, axis=1))
    done = [
        (matmul(p, stacked(v[c], masks)) / matmul(p, ones)).astype(BF16)
        for p, c in zip(weights, cuts)
    ]
    return jnp.concatenate(done, axis=0)


def attention_block(
    x, left, right, qkv_ref, ctx_ref, ones_ref, length, bias_of, gain, hook=None
):
    width = x.shape[1]
    qk = matmul(x, left).astype(BF16)
    v = matmul(x, right[:, :width]).astype(BF16)
    if length <= 128:
        ctx = attend_all(x, qk, v, length, bias_of, ones_ref[...], hook)
    else:
        if hook is not None:
            hook()
        qkv_ref[0] = qk[:, :width]
        qkv_ref[1] = qk[:, width:]
        qkv_ref[2] = v

        @pl.loop(0, x.shape[0] // length)
        def _(i):
            rows = pl.ds(pl.multiple_of(i * length, length), length)
            ctx_ref[rows, :] = attend(
                qkv_ref[0, rows, :],
                qkv_ref[1, rows, :],
                qkv_ref[2, rows, :],
                bias_of(i),
                ones_ref[...],
            )

        ctx = ctx_ref[...]
    update = matmul(ctx, right[:, width:])
    return normalize(x.astype(F32) + update, gain).astype(BF16)


def kernel(
    sizes,
    counts_hbm,
    train_hbm,
    gain_hbm,
    cells_hbm,
    fi_hbm,
    fo_hbm,
    si_hbm,
    so_hbm,
    hu_hbm,
    hd_hbm,
    out_hbm,
    counts_ref,
    train_ref,
    gain_ref,
    cells_ref,
    x_ref,
    fi_ref,
    fo_ref,
    si_ref,
    so_ref,
    hu_ref,
    hd_ref,
    wf,
    ws,
    wb,
    qkv,
    ctx,
    pick_send,
    pick_column,
    pick_row,
    feature_ones,
    sample_ones,
    send1,
    recv1,
    send2,
    recv2,
    ready,
    sa,
    ra,
    sb,
    rb,
    sz,
    rz,
    sp,
    sm,
    rm,
    cell_sems,
    load_sems,
    out_sems,
):
    wide, narrow = sizes
    total = wide * narrow
    chips = wide // 2
    g = lax.axis_index("groups")
    w = lax.axis_index("wide")
    n = lax.axis_index("narrow")
    me = w * narrow + n
    core = lax.rem(w, 2)
    chip = w // 2
    mate = w + 1 - 2 * core
    rows, width, feats = cells_ref.shape
    local = feats // total
    hl = local // 2
    pair = rows // 2
    piece = pair * hl
    all_rows = rows * total
    half_cells = rows * feats // 2

    barrier = pltpu.get_barrier_semaphore()
    for step in range(1, narrow):
        pl.semaphore_signal(
            barrier, inc=1, device_id=(g, w, lax.rem(n + step, narrow)), device_id_type=MESH
        )
    for step in range(1, wide):
        pl.semaphore_signal(
            barrier, inc=1, device_id=(g, lax.rem(w + step, wide), n), device_id_type=MESH
        )

    loads = [
        pltpu.make_async_copy(src, dst, load_sems.at[i])
        for i, (src, dst) in enumerate(
            (
                (fi_hbm, fi_ref),
                (fo_hbm, fo_ref),
                (cells_hbm, cells_ref),
                (si_hbm, si_ref),
                (so_hbm, so_ref),
                (hu_hbm, hu_ref),
                (hd_hbm, hd_ref),
                (gain_hbm, gain_ref),
                (counts_hbm, counts_ref),
                (train_hbm, train_ref),
            )
        )
    ]
    for load in loads:
        load.start()
    double = 2 * width
    shard = fi_ref.shape[0]
    loads[0].wait()
    loads[1].wait()
    wf[n, 0] = fi_ref[:, :double]
    wf[n, 1] = jnp.concatenate([fi_ref[:, double:], fo_ref[...]], axis=1)
    pl.semaphore_wait(barrier, narrow - 1 + wide - 1)

    weights = (wf, ws)
    steps = range(1, narrow)

    def along(group, step):
        ref = weights[group]
        return pltpu.make_async_remote_copy(
            src_ref=ref.at[n, core],
            dst_ref=ref.at[n, core],
            send_sem=sa.at[group, step],
            recv_sem=ra.at[group, step],
            device_id=(g, w, lax.rem(n + step, narrow)),
            device_id_type=MESH,
        )

    def across(group, step):
        ref = weights[group]
        owner = lax.rem(n - step + narrow, narrow)
        return pltpu.make_async_remote_copy(
            src_ref=ref.at[owner, core],
            dst_ref=ref.at[owner, core],
            send_sem=sb.at[group, step],
            recv_sem=rb.at[group, step],
            device_id=(g, mate, n),
            device_id_type=MESH,
        )

    def big(slot, step):
        block = core + 2 * slot
        return pltpu.make_async_remote_copy(
            src_ref=wb.at[n, block],
            dst_ref=wb.at[n, block],
            send_sem=sz.at[slot, step],
            recv_sem=rz.at[slot, step],
            device_id=(g, w, lax.rem(n + step, narrow)),
            device_id_type=MESH,
        )

    def spread(slot, step, to):
        block = core + 2 * slot
        owner = lax.rem(n - step + narrow, narrow)
        return pltpu.make_async_remote_copy(
            src_ref=wb.at[owner, block],
            dst_ref=wb.at[owner, block],
            send_sem=sp.at[slot, step, to],
            recv_sem=rz.at[slot, step],
            device_id=(g, lax.rem(w + 2 * to, wide), n),
            device_id_type=MESH,
        )

    def shared(slot, step):
        block = core + 2 * slot
        owner = lax.rem(n - step + narrow, narrow)
        return pltpu.make_async_remote_copy(
            src_ref=wb.at[owner, block],
            dst_ref=wb.at[owner, block],
            send_sem=sm.at[slot, step],
            recv_sem=rm.at[slot, step],
            device_id=(g, mate, n),
            device_id_type=MESH,
        )

    for step in steps:
        along(0, step).start()
    for step in steps:
        pl.semaphore_signal(
            ready, inc=1, device_id=(g, w, lax.rem(n + step, narrow)), device_id_type=MESH
        )

    for load in loads[3:7]:
        load.wait()
    ws[n, 0] = si_ref[:, :double]
    ws[n, 1] = jnp.concatenate([si_ref[:, double:], so_ref[...]], axis=1)
    wb[n, 0] = hu_ref[:, :double]
    wb[n, 1] = hu_ref[:, double:]
    down = hd_ref[...].astype(F32)
    for i in range(2):
        top = down[2 * i * shard : (2 * i + 1) * shard]
        low = down[(2 * i + 1) * shard : (2 * i + 2) * shard]
        wb[n, 2 + i] = jnp.concatenate([top, low], axis=1).astype(BF16)
    loads[2].wait()
    for r in range(rows):
        x_ref[r * feats : (r + 1) * feats, :] = cells_ref[r].astype(F32).T.astype(BF16)

    def to_send(i):
        h, k = i // (half_cells // 2), i % (half_cells // 2)
        d, r, j = k // piece, (k % piece) // hl, k % hl
        return r * feats + d * local + h * hl + j

    def to_column(i):
        j, k = i // all_rows, i % all_rows
        s, r = k // rows, k % rows
        return (r // pair) * (total * piece) + s * piece + (r % pair) * hl + j

    def to_row(j):
        def source(i):
            r, f = i // feats, i % feats
            d, h, at = f // local, (f % local) // hl, f % hl
            k = h * all_rows + d * rows + r
            return jnp.where(at == j, k, -1)

        return source

    prepare(pick_send, to_send)
    prepare(pick_column, to_column)
    for j in range(hl):
        prepare(pick_row.at[j], to_row(j))
    head_ones(feature_ones, feats)
    head_ones(sample_ones, all_rows)
    for load in loads[7:]:
        load.wait()

    for step in steps:
        along(0, step).wait_recv()
        across(0, step).start()
    for step in steps:
        along(1, step).start()
    for step in steps:
        across(0, step).wait_recv()

    def flipped(value, bits):
        at = 1
        for _ in range(bits.bit_length()):
            if bits & at:
                value = value + at * (1 - 2 * lax.rem(value // at, 2))
            at *= 2
        return value

    def copy_to(send, recv, index, part, tw, tn):
        return pltpu.make_async_remote_copy(
            src_ref=send.at[part, tw * narrow + tn],
            dst_ref=recv.at[part, me],
            send_sem=cell_sems.at[index, 0, part],
            recv_sem=cell_sems.at[index, 1, part],
            device_id=(g, tw, tn),
            device_id_type=MESH,
        )

    others = [
        (flipped(w, a), flipped(n, b))
        for b in reversed(range(narrow))
        for a in reversed(range(wide))
        if total <= 32 and (a or b)
    ]

    def exchange(send, recv, index, part):
        recv[part, me] = send[part, me]
        if total <= 32:
            for tw, tn in others:
                copy_to(send, recv, index, part, tw, tn).start()
        else:
            @pl.loop(1, total)
            def _(step):
                to = lax.rem(me + step, total)
                copy_to(send, recv, index, part, to // narrow, lax.rem(to, narrow)).start()

    def exchanged(ref, index, way, part):
        whole = ref.at[part, pl.ds(0, total - 1)]
        pltpu.make_async_copy(whole, whole, cell_sems.at[index, way, part]).wait()

    keys = lax.broadcasted_iota(jnp.int32, (1, feats), 1)
    left, right = gathered(wf, 0), gathered(wf, 1)
    for q in range(2):
        x = x_ref[q * half_cells : (q + 1) * half_cells, :]
        first = attention_block(
            x,
            left,
            right,
            qkv,
            ctx,
            feature_ones,
            feats,
            lambda i: jnp.where(keys < counts_ref[q * pair + i], 0.0, -1e30),
            gain_ref[0:1, :],
            None,
        )
        picked = reorder(pick_send, first)
        both = jnp.concatenate([picked[: half_cells // 2], picked[half_cells // 2 :]], axis=1)
        send1[q] = both.reshape(total, piece, double).astype(BF16)
        if q == 0:
            pl.semaphore_wait(ready, narrow - 1)
        exchange(send1, recv1, 0, q)

    for step in steps:
        along(1, step).wait_recv()
        across(1, step).start()
    for slot in range(2):
        @pl.when(chip == core + 2 * slot)
        def _(slot=slot):
            for step in steps:
                big(slot, step).start()
    for step in steps:
        across(1, step).wait_recv()
    left, right = gathered(ws, 0), gathered(ws, 1)
    for q in range(2):
        exchanged(recv1, 0, 1, q)
    for slot in range(2):
        @pl.when(chip == core + 2 * slot)
        def _(slot=slot):
            for step in steps:
                big(slot, step).wait_recv()
                for to in range(1, chips):
                    spread(slot, step, to).start()
                shared(slot, step).start()

    samples = lax.broadcasted_iota(jnp.int32, (1, all_rows), 1)
    sample_bias = jnp.where(samples < train_ref[0], 0.0, -1e30)
    landed = jnp.concatenate(
        [recv1[q].astype(F32).reshape(total * piece, double).astype(BF16) for q in range(2)], axis=0
    )
    for j in range(hl):
        y = reorder(pick_column, landed, j * all_rows, all_rows).astype(BF16)
        y = jnp.concatenate([y[:, :width], y[:, width:]], axis=0)
        second = attention_block(
            y, left, right, qkv, ctx, sample_ones, all_rows, lambda i: sample_bias, gain_ref[1:2, :]
        )
        done = jnp.concatenate([second[:all_rows, :], second[all_rows:, :]], axis=1)
        send2[j] = done.astype(F32).reshape(total, rows, double).astype(BF16)
        exchange(send2, recv2, 1, j)

    for slot in range(2):
        @pl.when(chip != core + 2 * slot)
        def _(slot=slot):
            for step in steps:
                big(slot, step).wait_recv()
                shared(slot, step).start()

    for step in steps:
        for group in range(2):
            along(group, step).wait_send()
            across(group, step).wait_send()
        for slot in range(2):
            @pl.when(chip == core + 2 * slot)
            def _(slot=slot, step=step):
                big(slot, step).wait_send()
                for to in range(1, chips):
                    spread(slot, step, to).wait_send()

            shared(slot, step).wait_send()
    for q in range(2):
        exchanged(send1, 0, 0, q)

    tile = min(512, half_cells)
    parts = []
    for step in steps:
        for slot in range(2):
            shared(slot, step).wait_recv()
    up = [gathered(wb, c) for c in range(2)]
    low = gathered_down(wb, width)

    def feed(values):
        halves = []
        for c in range(2):
            h = matmul(values, up[c])
            halves.append((0.5 * h * (1.0 + lax.erf(h * (2.0**-0.5)))).astype(BF16))
        back = matmul(jnp.concatenate(halves, axis=1), low)
        return normalize(values.astype(F32) + back, gain_ref[2:3, :]).astype(BF16)

    for j in range(hl):
        exchanged(recv2, 1, 1, j)
        both = recv2[j].astype(F32).reshape(all_rows, double).astype(BF16)
        values = jnp.concatenate([both[:, :width], both[:, width:]], axis=0)
        if half_cells == tile:
            parts.append(feed(values))
            continue
        ctx[...] = values

        @pl.loop(0, half_cells // tile)
        def _(i):
            at = pl.ds(pl.multiple_of(i * tile, tile), tile)
            ctx[at, :] = feed(ctx[at, :])

        parts.append(ctx[...])
    for r in range(rows):
        ordered = sum(reorder(pick_row.at[j], parts[j], r * feats, feats) for j in range(hl))
        out_hbm[r] = ordered.T.astype(BF16)
    for j in range(hl):
        exchanged(send2, 1, 0, j)


def body(sizes, cells, counts, train, gain, fi, fo, si, so, hu, hd):
    wide, narrow = sizes
    total = wide * narrow
    cells = jnp.swapaxes(cells, 1, 2)
    rows, width, feats = cells.shape
    hl = feats // total // 2
    pair = rows // 2
    half = rows * feats // 2
    all_rows = rows * total
    shard = fi.shape[0]
    anywhere = pl.BlockSpec(memory_space=pl.ANY)
    sems = pltpu.SemaphoreType.DMA((2, narrow))
    weight = pltpu.VMEM((narrow, 2, shard, 2 * width), BF16)
    first = pltpu.VMEM((2, total, pair * hl, 2 * width), BF16)
    last = pltpu.VMEM((hl, total, rows, 2 * width), BF16)
    out = pl.pallas_call(
        functools.partial(kernel, sizes),
        out_shape=pltpu.VMEM(cells.shape, BF16),
        in_specs=[pl.BlockSpec(memory_space=pltpu.HBM)] * 10,
        out_specs=pl.BlockSpec(memory_space=pltpu.VMEM),
        scratch_shapes=[
            pltpu.SMEM(counts.shape, jnp.int32),
            pltpu.SMEM(train.shape, jnp.int32),
            pltpu.VMEM(gain.shape, F32),
            pltpu.VMEM(cells.shape, BF16),
            pltpu.VMEM((rows * feats, width), BF16),
            *[pltpu.VMEM(a.shape, BF16) for a in (fi, fo, si, so, hu, hd)],
            weight,
            weight,
            pltpu.VMEM((narrow, 4, shard, 2 * width), BF16),
            pltpu.VMEM((3, half, width), BF16),
            pltpu.VMEM((half, width), BF16),
            pltpu.VMEM((half, half), BF16),
            pltpu.VMEM((hl * all_rows, half), BF16),
            pltpu.VMEM((hl, rows * feats, half), BF16),
            pltpu.VMEM((HEADS * feats, width), BF16),
            pltpu.VMEM((HEADS * all_rows, width), BF16),
            first,
            first,
            last,
            last,
            pltpu.SemaphoreType.REGULAR,
            sems,
            sems,
            sems,
            sems,
            sems,
            sems,
            pltpu.SemaphoreType.DMA((2, narrow, wide // 2)),
            sems,
            sems,
            pltpu.SemaphoreType.DMA((2, 2, 2)),
            pltpu.SemaphoreType.DMA((10,)),
            pltpu.SemaphoreType.DMA((rows,)),
        ],
        compiler_params=pltpu.CompilerParams(
            collective_id=0, has_side_effects=True, vmem_limit_bytes=56 << 20
        ),
    )(counts, train, gain, cells, fi, fo, si, so, hu, hd)
    return jnp.swapaxes(out, 1, 2)


def solution(mesh):
    sizes = (mesh.shape["wide"], mesh.shape["narrow"])
    return jax.shard_map(
        functools.partial(body, sizes),
        mesh=mesh,
        in_specs=(
            P(("groups", "wide", "narrow"), None, None),
            P(("groups", "wide", "narrow")),
            P("groups"),
            P(),
            P("narrow", None),
            P("narrow", None),
            P("narrow", None),
            P("narrow", None),
            P("narrow", None),
            P("narrow", None),
        ),
        out_specs=P(("groups", "wide", "narrow"), None, None),
        check_vma=False,
    )
```
